512 devices in a mesh: dp: 64 (over y, z), fsdp: 8 (over x, core).
Axes of the slice: x: 4, y: 8, z: 8, core: 2. Of those that a mesh axis runs over, the one named last changes fastest.
Arguments:
- frames: bfloat16 [524288, 512], P(('dp', 'fsdp')), may hold values from -6 to 6
- utt_pairs: int32 [8, 64, 4], P('fsdp'), may hold values from 32 to 256, as said below
- utt_dest: int32 [8, 64, 4], P('fsdp'), may hold values from 0 to 63, as said below
- conv_weight: bfloat16 [1536, 512], P('dp'), may hold values from -0.15625 to 0.15625
- proj_weight: bfloat16 [512, 1536], P('dp'), may hold values from -0.25 to 0.25
- point_weight: bfloat16 [2, 1536, 1536], P(None, None, 'fsdp'), may hold values from -0.15625 to 0.15625
- depth_weight: float32 [31, 1536], replicated, may hold values from -1 to 1
- gain_first: float32 [1536], replicated, may hold values from 0.5 to 1.5
- gain_second: float32 [1536], replicated, may hold values from 0.5 to 1.5
Outputs:
- encoded: bfloat16 [262144, 1536], P(('dp', 'fsdp'))
The draws below stay inside these ranges and needn't reach their ends.
Inputs may be any that keep to these rules, and one draw needn't show every extreme that they name: `utt_pairs`: every loader holds exactly 512 pairs and every sequence device receives exactly 512 pairs, from 4 different loaders. Each loader holds one utterance of exactly 256 pairs and one of exactly 32 pairs. `utt_dest`: the 4 utterances of loader i go to the 4 different sequence devices (i + k * 64 / 4) mod 64, k = 0 .. 3, in some order.
All inputs are finite; a program needn't handle non-finite values.
Results may differ from the reference program's by a relative error of at most 0.012.
Values may be sent and summed in bfloat16 or wider, within the bound.
No kernel may reach another device: no remote copies, remote signals or barrier semaphores. Data moves between devices by JAX's collectives and lax.ppermute only.
A program may use at most 64 MiB of HBM per device.

```python
import jax
import jax.numpy as jnp
from jax import lax

CONV_CH = 512
WIDTH = 1536
KERNEL = 31
UTTS = 4
PAIRS = 512
SLOT = 256
N_DP = 64
N_FSDP = 8


def packing_plan(key):
    spacing = N_DP // UTTS

    def one_group(group_key):
        subkeys = jax.random.split(group_key, 3)
        shortest = PAIRS // 16
        extra = jax.random.randint(subkeys[0], (spacing,), 0, 5 * PAIRS // 16 + 1).astype(jnp.int32)
        third = (shortest + extra).astype(jnp.int32)
        fourth = (PAIRS - SLOT - shortest - third).astype(jnp.int32)
        longest = jnp.full((spacing,), SLOT, jnp.int32)
        short_col = jnp.full((spacing,), shortest, jnp.int32)
        base = jnp.stack([longest, short_col, third, fourth], axis=1).astype(jnp.int32)

        def one_perm(perm_key):
            return jax.random.permutation(perm_key, UTTS).astype(jnp.int32)
        class_perm = jax.vmap(one_perm)(jax.random.split(subkeys[1], spacing))
        listed = jnp.take_along_axis(base, class_perm, axis=1)
        loader_perm = jax.vmap(one_perm)(jax.random.split(subkeys[2], N_DP))
        loaders = jnp.arange(N_DP, dtype=jnp.int32)
        destinations = (loaders[:, None] + loader_perm * spacing) % N_DP
        pair_table = jnp.take_along_axis(listed[loaders % spacing], loader_perm, axis=1)
        return (pair_table.astype(jnp.int32), destinations.astype(jnp.int32))
    return jax.vmap(one_group)(jax.random.split(jax.random.fold_in(key, 7), N_FSDP))


def draw_utt_pairs(key, part):
    return packing_plan(key)[0]


def draw_utt_dest(key, part):
    return packing_plan(key)[1]


def steps_of(own_key, extent, cuts, least, top_value):
    def one(axis_at, parts):
        steps = jax.random.uniform(jax.random.fold_in(jax.random.fold_in(own_key, 6), axis_at), (parts,), jnp.float32, least / len(cuts), top_value / len(cuts))
        return jnp.repeat(jnp.exp(steps), extent[axis_at] // parts).reshape((-1,) + (1,) * (len(extent) - axis_at - 1))

    factor_of = one(*cuts[0])
    for cut in cuts[1:]:
        factor_of = factor_of * one(*cut)
    return factor_of


def bell_draw(stream_key, shape, spread, limit, cuts=(), kind=jnp.bfloat16):
    values = jax.random.normal(stream_key, shape, jnp.float32) * spread
    if len(cuts) > 0:
        values = steps_of(stream_key, shape, cuts, -0.22, 0.18) * values
    return jnp.clip(values, min=-limit, max=limit).astype(kind)


def setup_inputs(seed: int = 0) -> dict:
    arg_keys = jax.random.split(jax.random.key(seed), 10)
    return {
        "frames": bell_draw(arg_keys[0], (N_DP * N_FSDP * 2 * PAIRS, CONV_CH), 1.0, 6.0, ((0, 512),)),
        "utt_pairs": draw_utt_pairs(jax.random.fold_in(arg_keys[9], 71), 0),
        "utt_dest": draw_utt_dest(jax.random.fold_in(arg_keys[9], 71), 0),
        "conv_weight": bell_draw(arg_keys[3], (3 * CONV_CH, CONV_CH), (3 * CONV_CH) ** -0.5, 0.15625, ((0, 64),)),
        "proj_weight": bell_draw(arg_keys[4], (CONV_CH, WIDTH), CONV_CH ** -0.5, 0.25, ((0, 64),)),
        "point_weight": bell_draw(arg_keys[5], (2, WIDTH, WIDTH), WIDTH ** -0.5, 0.15625, ((2, 8),)),
        "depth_weight": bell_draw(arg_keys[6], (KERNEL, WIDTH), KERNEL ** -0.5, 1.0, (), jnp.float32),
        "gain_first": jnp.clip(1.0 + 0.1 * jax.random.normal(arg_keys[7], (WIDTH,), jnp.float32), 0.5, 1.5),
        "gain_second": jnp.clip(1.0 + 0.1 * jax.random.normal(arg_keys[8], (WIDTH,), jnp.float32), 0.5, 1.5),
    }


def packing_tables(pair_table, dest_table, node_count):
    targets = jnp.arange(node_count, dtype=jnp.int32)
    matches = (dest_table[:, :, None] == targets[None, None, :]).astype(jnp.int32)
    loader_offsets = (jnp.cumsum(pair_table, axis=1) - pair_table).astype(jnp.int32)
    counts = lax.optimization_barrier(jnp.sum(matches * pair_table[:, :, None], axis=1)).astype(jnp.int32)
    starts = lax.optimization_barrier(jnp.sum(matches * loader_offsets[:, :, None], axis=1)).astype(jnp.int32)
    return (counts, starts)

def packed_positions(column, pair_count):
    column_offsets = (jnp.cumsum(column) - column).astype(jnp.int32)
    pair_rows = jnp.arange(pair_count, dtype=jnp.int32)
    source = (lax.optimization_barrier(jnp.sum((column_offsets[None, :] <= pair_rows[:, None]).astype(jnp.int32), axis=1)) - 1).astype(jnp.int32)
    positions = (pair_rows - jnp.take(column_offsets, source)).astype(jnp.int32)
    lengths = jnp.take(column, source).astype(jnp.int32)
    return (source, positions, lengths)

def frontend(pair_rows, first_rows, conv_full):
    channels = pair_rows.shape[1] // 2
    even_frames = pair_rows[:, :channels]
    odd_frames = pair_rows[:, channels:]
    earlier = jnp.pad(odd_frames[:-1], ((1, 0), (0, 0)))
    earlier = jnp.where(first_rows[:, None], jnp.zeros_like(earlier), earlier)
    summed = jnp.dot(earlier, conv_full[:channels], preferred_element_type=jnp.float32)
    summed = summed + jnp.dot(even_frames, conv_full[channels:2 * channels], preferred_element_type=jnp.float32)
    summed = summed + jnp.dot(odd_frames, conv_full[2 * channels:], preferred_element_type=jnp.float32)
    return jax.nn.relu(summed).astype(jnp.bfloat16)

def layer_norm(values, scales):
    centered = values - lax.optimization_barrier(jnp.mean(values, axis=-1, keepdims=True))
    variance = lax.optimization_barrier(jnp.mean(centered * centered, axis=-1, keepdims=True))
    return centered * lax.rsqrt(variance + 1e-05) * scales

def depthwise(gated, depth_weight, positions, lengths):
    row_count = gated.shape[0]
    kernel_size = depth_weight.shape[0]
    half_width = kernel_size // 2
    padded = jnp.pad(gated.astype(jnp.float32), ((half_width, half_width), (0, 0)))
    mixed = jnp.zeros(gated.shape, jnp.float32)
    for tap_index in range(kernel_size):
        offset = tap_index - half_width
        inside = (positions + offset >= 0) & (positions + offset < lengths)
        term = padded[tap_index:tap_index + row_count] * depth_weight[tap_index][None, :]
        mixed = mixed + jnp.where(inside[:, None], term, jnp.zeros_like(term))
    return mixed

def reference(frames, utt_pairs, utt_dest, conv_weight, proj_weight, point_weight, depth_weight, gain_first, gain_second):
    frame_pairs = frames.reshape(N_DP * N_FSDP * PAIRS, 2 * CONV_CH)

    def group_tables(pair_table, dest_table):
        return packing_tables(pair_table, dest_table, N_DP)
    counts_all, starts_all = jax.vmap(group_tables)(utt_pairs, utt_dest)

    def one_sequence(sequence_id):
        device_dp = sequence_id // N_FSDP
        group_index = sequence_id % N_FSDP
        counts = counts_all[group_index]
        starts = starts_all[group_index]
        column = counts[:, device_dp]
        source, positions, lengths = packed_positions(column, PAIRS)
        global_rows = (source * N_FSDP + group_index) * PAIRS + jnp.take(starts[:, device_dp], source) + positions
        packed = jnp.take(frame_pairs, global_rows.astype(jnp.int32), axis=0)
        front = frontend(packed, positions == 0, conv_weight)
        projected = jnp.dot(front, proj_weight, preferred_element_type=jnp.float32).astype(jnp.bfloat16)
        normed = layer_norm(projected.astype(jnp.float32), gain_first).astype(jnp.bfloat16)
        value_part = jnp.dot(normed, point_weight[0], preferred_element_type=jnp.float32)
        gate_part = jnp.dot(normed, point_weight[1], preferred_element_type=jnp.float32)
        gated = (value_part * jax.nn.sigmoid(gate_part)).astype(jnp.bfloat16)
        mixed = depthwise(gated, depth_weight, positions, lengths)
        scaled = layer_norm(mixed, gain_second)
        return (scaled * jax.nn.sigmoid(scaled)).astype(jnp.bfloat16)
    results = lax.map(one_sequence, jnp.arange(N_DP * N_FSDP, dtype=jnp.int32))
    return results.reshape(N_DP * N_FSDP * PAIRS, WIDTH)
```

```python
import functools

import jax
import jax.numpy as jnp
from jax import lax
from jax.experimental import pallas as pl
from jax.experimental.pallas import tpu as pltpu
from jax.sharding import PartitionSpec as P

GAP = 16
BF16 = jnp.bfloat16
F32 = jnp.float32


def shifted(value, axis, steps):
    count = lax.axis_size(axis)
    pairs = [(source, (source + steps) % count) for source in range(count)]
    return lax.ppermute(value, axis, pairs)


def core_swapped(value, axis):
    count = lax.axis_size(axis)
    return lax.ppermute(value, axis, [(j, j ^ 1) for j in range(count)])


def spread(value, axis, groups):
    size = len(groups[0])
    copies = jnp.broadcast_to(value[None], (size,) + value.shape)
    return lax.all_to_all(copies, axis, 0, 0, axis_index_groups=groups)


def as_bf16(mask):
    return jnp.where(mask, 1.0, 0.0).astype(BF16)


def iota(shape, axis):
    return lax.broadcasted_iota(jnp.int32, shape, axis)


def arriving(own, pair_ref, dest_ref, node_count):
    utts = pair_ref.shape[0]
    spacing = node_count // utts
    sources, lengths = [], []
    for slot in range(utts):
        source = lax.rem(own + node_count - slot * spacing, node_count)
        length = jnp.int32(0)
        for utt in range(utts):
            length += jnp.where(dest_ref[utt, source] == own, pair_ref[utt, source], 0)
        sources.append(source)
        lengths.append(length)
    starts, padded_starts = [], []
    for slot in range(utts):
        start, padded_start = jnp.int32(0), jnp.int32(0)
        for other in range(utts):
            if other != slot:
                before = sources[other] < sources[slot]
                start += jnp.where(before, lengths[other], 0)
                padded_start += jnp.where(before, lengths[other] + GAP, 0)
        starts.append(start)
        padded_starts.append(padded_start)
    return lengths, starts, padded_starts


def cut_kernel(node_count, place_ref, pair_ref, dest_ref, frames_ref, *out_refs):
    own = place_ref[0]
    utts = len(out_refs)
    spacing = node_count // utts
    slot_rows = out_refs[0].shape[0]
    frame_count, channels = frames_ref.shape
    offset = jnp.int32(0)
    starts = [jnp.int32(0)] * utts
    for utt in range(utts):
        for slot in range(utts):
            target = lax.rem(own + slot * spacing, node_count)
            starts[slot] += jnp.where(dest_ref[utt, own] == target, offset, 0)
        offset += pair_ref[utt, own]
    shape = (slot_rows, frame_count)
    ahead = iota(shape, 1) - 2 * iota(shape, 0)
    for slot in range(utts):
        for parity in range(2):
            chosen = as_bf16(ahead == 2 * starts[slot] + parity)
            rows = jnp.dot(chosen, frames_ref[...], preferred_element_type=F32)
            out_refs[slot][:, parity * channels : (parity + 1) * channels] = rows.astype(BF16)


def pack_kernel(node_count, place_ref, pair_ref, dest_ref, *refs):
    piece_refs, out_ref = refs[:-1], refs[-1]
    rows = out_ref.shape[0]
    slot_rows, width = piece_refs[0].shape
    channels = width // 2
    lengths, _, padded_starts = arriving(place_ref[0], pair_ref, dest_ref, node_count)
    shape = (rows, slot_rows)
    behind = iota(shape, 0) - iota(shape, 1)
    within = iota(shape, 1)
    both = jnp.zeros((rows, width), F32)
    earlier = jnp.zeros((rows, channels), F32)
    for slot, piece_ref in enumerate(piece_refs):
        here = as_bf16((behind == padded_starts[slot]) & (within < lengths[slot]))
        both += jnp.dot(here, piece_ref[...], preferred_element_type=F32)
        later = as_bf16((behind == padded_starts[slot] + 1) & (within < lengths[slot] - 1))
        earlier += jnp.dot(later, piece_ref[:, channels:], preferred_element_type=F32)
    out_ref[:, :channels] = earlier.astype(BF16)
    out_ref[:, channels:] = both.astype(BF16)


def layer_norm(values, scales):
    centered = values - jnp.mean(values, axis=-1, keepdims=True)
    variance = jnp.mean(centered * centered, axis=-1, keepdims=True)
    return centered * lax.rsqrt(variance + 1e-05) * scales


def front_kernel(place_ref, xs_ref, parts_ref, gain_ref, out_ref, conv_ref, proj_ref):
    count, part_rows, lanes = parts_ref.shape
    half = count // 2
    chips = count // 2
    position = place_ref[1]
    chip, core = position // 2, lax.rem(position, 2)

    def part(index):
        away = lax.rem(index // 2 + chips - chip, chips)
        other_core = jnp.where(core == index % 2, 0, chips)
        return parts_ref[away + other_core]

    tiles = proj_ref.shape[1] // (half * lanes)
    for index in range(half):
        conv_ref[:, index * lanes : (index + 1) * lanes] = part(index)
    blocks = part_rows // (8 * tiles)
    for index in range(half):
        split = part(half + index).astype(F32).reshape(blocks, tiles, 8, lanes)
        for tile in range(tiles):
            at = (index * tiles + tile) * lanes
            piece = split[:, tile].reshape(blocks * 8, lanes)
            proj_ref[:, at : at + lanes] = piece.astype(BF16)
    front = jnp.dot(xs_ref[...], conv_ref[...], preferred_element_type=F32)
    front = jnp.maximum(front, 0.0).astype(BF16)
    projected = jnp.dot(front, proj_ref[...], preferred_element_type=F32)
    projected = projected.astype(BF16).astype(F32)
    out_ref[...] = layer_norm(projected, gain_ref[...]).astype(BF16)


def mix_kernel(
    node_count,
    place_ref,
    pair_ref,
    dest_ref,
    normed_ref,
    weight_ref,
    depth_ref,
    gain_ref,
    out_ref,
    gated_ref,
    mixed_ref,
):
    step = pl.program_id(0)
    rows = normed_ref.shape[0]
    block = weight_ref.shape[1]
    taps = depth_ref.shape[0]
    contract = (((1,), (1,)), ((), ()))
    value = lax.dot_general(
        normed_ref[...], weight_ref[0], contract, preferred_element_type=F32
    )
    gate = lax.dot_general(
        normed_ref[...], weight_ref[1], contract, preferred_element_type=F32
    )
    gated_ref[pl.ds(0, GAP), :] = jnp.zeros((GAP, block), F32)
    gated_ref[pl.ds(GAP + rows, GAP), :] = jnp.zeros((GAP, block), F32)
    gated = (value * jax.nn.sigmoid(gate)).astype(BF16)
    gated_ref[pl.ds(GAP, rows), :] = gated.astype(F32)
    span = 56
    for lane in range(0, block, 128):
        lanes = slice(lane, lane + 128)
        for row in range(0, rows, span):
            near = gated_ref[row : row + span + 32, lanes]
            total = None
            for low in range(7, -1, -1):
                partial = None
                for high in range(0, 32, 8):
                    tap = high + low - 1
                    if 0 <= tap < taps:
                        term = near[high : high + span + 8] * depth_ref[tap : tap + 1, lanes]
                        partial = term if partial is None else partial + term
                if total is None:
                    total = partial
                else:
                    total = partial + pltpu.roll(total, span + 7, 0)
            at = pl.multiple_of(step * block + lane, 128)
            mixed_ref[row : row + span, pl.ds(at, 128)] = total[:span]

    @pl.when(step == pl.num_programs(0) - 1)
    def _():
        scaled = layer_norm(mixed_ref[...], gain_ref[...])
        encoded = (scaled * jax.nn.sigmoid(scaled)).astype(BF16)
        _, starts, _ = arriving(place_ref[0], pair_ref, dest_ref, node_count)
        out_rows = out_ref.shape[0]
        shape = (out_rows, rows)
        row_ids = iota(shape, 0)
        target = row_ids - GAP
        for start in starts:
            target += jnp.where(row_ids >= start, GAP, 0)
        chosen = as_bf16(iota(shape, 1) == target)
        out_ref[...] = jnp.dot(chosen, encoded, preferred_element_type=F32).astype(BF16)


SMEM = pl.BlockSpec(memory_space=pltpu.SMEM)
VMEM = pl.BlockSpec(memory_space=pltpu.VMEM)


def params():
    return pltpu.CompilerParams(vmem_limit_bytes=40 * 2**20)


def body(
    frames,
    utt_pairs,
    utt_dest,
    conv_weight,
    proj_weight,
    point_weight,
    depth_weight,
    gain_first,
    gain_second,
):
    node_count = lax.axis_size("dp")
    position = lax.axis_index("fsdp")
    frame_count, channels = frames.shape
    pair_count = frame_count // 2
    utts = utt_pairs.shape[2]
    spacing = node_count // utts
    slot_rows = pair_count // 2
    width = proj_weight.shape[1]
    place = jnp.stack([lax.axis_index("dp"), position]).astype(jnp.int32)
    pair_table = utt_pairs[0].T
    dest_table = utt_dest[0].T
    rows = pair_count + (utts - 1) * GAP

    weight_rows = jnp.swapaxes(point_weight, 1, 2)
    weight_full = lax.all_gather(weight_rows, "fsdp", axis=1, tiled=True)

    pieces = pl.pallas_call(
        functools.partial(cut_kernel, node_count),
        out_shape=[jax.ShapeDtypeStruct((slot_rows, 2 * channels), BF16)] * utts,
        in_specs=[SMEM, SMEM, SMEM, VMEM],
        out_specs=[VMEM] * utts,
        compiler_params=params(),
        name="cut",
    )(place, pair_table, dest_table, frames)
    arrived = [pieces[0]]
    for slot in range(1, utts):
        arrived.append(shifted(pieces[slot], "dp", slot * spacing))

    half = 4
    lanes = channels // half
    conv_split = conv_weight.reshape(conv_weight.shape[0], half, lanes)
    conv_part = lax.dynamic_slice_in_dim(conv_weight, (position % half) * lanes, lanes, 1)
    proj_rows = proj_weight.shape[0]
    tiles = width // (half * lanes)
    proj_part = lax.dynamic_slice_in_dim(
        proj_weight, (position % half) * tiles * lanes, tiles * lanes, 1
    )
    proj_part = jnp.concatenate(
        [proj_part[:, t * lanes : (t + 1) * lanes] for t in range(tiles)], axis=0
    )
    own_part = jnp.where(position < half, conv_part, proj_part)
    side = 8
    y_groups = [[y * side + z for y in range(side)] for z in range(side)]
    z_groups = [[y * side + z for z in range(side)] for y in range(side)]
    piece_rows = own_part.shape[0]
    by_y = spread(own_part, "dp", y_groups).reshape(side * piece_rows, lanes)
    by_z = spread(by_y, "dp", z_groups)
    by_z = by_z.reshape(side, side, piece_rows, lanes).swapaxes(0, 1)
    mine = by_z.reshape(side * side * piece_rows, lanes)
    following = shifted(mine, "fsdp", -2)
    opposite = shifted(mine, "fsdp", 4)
    preceding = shifted(mine, "fsdp", 2)
    same = jnp.stack([mine, following, opposite, preceding])
    parts = jnp.concatenate([same, core_swapped(same, "fsdp")])

    packed = pl.pallas_call(
        functools.partial(pack_kernel, node_count),
        out_shape=jax.ShapeDtypeStruct((rows, 3 * channels), BF16),
        in_specs=[SMEM, SMEM, SMEM] + [VMEM] * utts,
        out_specs=VMEM,
        compiler_params=params(),
        name="pack",
    )(place, pair_table, dest_table, *arrived)
    normed = pl.pallas_call(
        front_kernel,
        out_shape=jax.ShapeDtypeStruct((rows, width), BF16),
        in_specs=[SMEM, VMEM, VMEM, VMEM],
        out_specs=VMEM,
        scratch_shapes=[
            pltpu.VMEM((3 * channels, channels), BF16),
            pltpu.VMEM((channels, width), BF16),
        ],
        compiler_params=params(),
        name="front",
    )(place, packed, parts, gain_first[None])

    block = 256
    taps = depth_weight.shape[0]
    return pl.pallas_call(
        functools.partial(mix_kernel, node_count),
        out_shape=jax.ShapeDtypeStruct((pair_count, width), BF16),
        grid=(width // block,),
        in_specs=[
            SMEM,
            SMEM,
            SMEM,
            pl.BlockSpec((rows, width), lambda n: (0, 0)),
            pl.BlockSpec((2, block, width), lambda n: (0, n, 0)),
            pl.BlockSpec((taps, block), lambda n: (0, n)),
            pl.BlockSpec((1, width), lambda n: (0, 0)),
        ],
        out_specs=pl.BlockSpec((pair_count, width), lambda n: (0, 0)),
        scratch_shapes=[
            pltpu.VMEM((rows + 2 * GAP, block), F32),
            pltpu.VMEM((rows, width), F32),
        ],
        compiler_params=params(),
        name="mix",
    )(place, pair_table, dest_table, normed, weight_full, depth_weight, gain_second[None])


def solution(mesh):
    in_specs = (
        P(("dp", "fsdp"), None),
        P("fsdp", None, None),
        P("fsdp", None, None),
        P("dp", None),
        P("dp", None),
        P(None, None, "fsdp"),
        P(),
        P(),
        P(),
    )
    out_specs = P(("dp", "fsdp"), None)
    return jax.shard_map(body, mesh=mesh, in_specs=in_specs, out_specs=out_specs, check_vma=False)
```

```python
import functools

import jax
import jax.numpy as jnp
from jax import lax
from jax.experimental import pallas as pl
from jax.experimental.pallas import tpu as pltpu
from jax.sharding import PartitionSpec as P

GAP = 16
BF16 = jnp.bfloat16
F32 = jnp.float32


def shifted(value, axis, steps):
    count = lax.axis_size(axis)
    pairs = [(source, (source + steps) % count) for source in range(count)]
    return lax.ppermute(value, axis, pairs)


def core_swapped(value, axis):
    count = lax.axis_size(axis)
    return lax.ppermute(value, axis, [(j, j ^ 1) for j in range(count)])


def along_z(value, side, steps):
    pairs = [
        (y * side + z, y * side + (z + steps) % side) for y in range(side) for z in range(side)
    ]
    return lax.ppermute(value, "dp", pairs)


def as_bf16(mask):
    return jnp.where(mask, 1.0, 0.0).astype(BF16)


def iota(shape, axis):
    return lax.broadcasted_iota(jnp.int32, shape, axis)


def arriving(own, pair_ref, dest_ref, node_count):
    utts = pair_ref.shape[0]
    spacing = node_count // utts
    sources, lengths = [], []
    for slot in range(utts):
        source = lax.rem(own + node_count - slot * spacing, node_count)
        length = jnp.int32(0)
        for utt in range(utts):
            length += jnp.where(dest_ref[utt, source] == own, pair_ref[utt, source], 0)
        sources.append(source)
        lengths.append(length)
    starts, padded_starts = [], []
    for slot in range(utts):
        start, padded_start = jnp.int32(0), jnp.int32(0)
        for other in range(utts):
            if other != slot:
                before = sources[other] < sources[slot]
                start += jnp.where(before, lengths[other], 0)
                padded_start += jnp.where(before, lengths[other] + GAP, 0)
        starts.append(start)
        padded_starts.append(padded_start)
    return lengths, starts, padded_starts


def own_kernel(place_ref, conv_ref, proj_ref, out_ref):
    copies, part_rows, lanes = out_ref.shape
    proj = proj_ref[...].astype(F32)
    tiles = [proj[:, at : at + lanes] for at in range(0, proj.shape[1], lanes)]
    is_conv = lax.rem(place_ref[1], 2) == 0
    chosen = jnp.where(is_conv, conv_ref[...].astype(F32), jnp.concatenate(tiles, axis=0))
    for copy in range(copies):
        out_ref[copy] = chosen.astype(BF16)


def cut_kernel(node_count, place_ref, pair_ref, dest_ref, frames_ref, *out_refs):
    own = place_ref[0]
    utts = len(out_refs)
    spacing = node_count // utts
    slot_rows = out_refs[0].shape[0]
    frame_count, channels = frames_ref.shape
    offset = jnp.int32(0)
    starts = [jnp.int32(0)] * utts
    for utt in range(utts):
        for slot in range(utts):
            target = lax.rem(own + slot * spacing, node_count)
            starts[slot] += jnp.where(dest_ref[utt, own] == target, offset, 0)
        offset += pair_ref[utt, own]
    shape = (slot_rows, frame_count)
    ahead = iota(shape, 1) - 2 * iota(shape, 0)
    for slot in range(utts):
        for parity in range(2):
            chosen = as_bf16(ahead == 2 * starts[slot] + parity)
            rows = jnp.dot(chosen, frames_ref[...], preferred_element_type=F32)
            out_refs[slot][:, parity * channels : (parity + 1) * channels] = rows.astype(BF16)


def pack_kernel(node_count, place_ref, pair_ref, dest_ref, *refs):
    piece_refs, out_ref = refs[:-1], refs[-1]
    rows = out_ref.shape[0]
    slot_rows, width = piece_refs[0].shape
    channels = width // 2
    lengths, _, padded_starts = arriving(place_ref[0], pair_ref, dest_ref, node_count)
    shape = (rows, slot_rows)
    behind = iota(shape, 0) - iota(shape, 1)
    within = iota(shape, 1)
    both = jnp.zeros((rows, width), F32)
    earlier = jnp.zeros((rows, channels), F32)
    for slot, piece_ref in enumerate(piece_refs):
        here = as_bf16((behind == padded_starts[slot]) & (within < lengths[slot]))
        both += jnp.dot(here, piece_ref[...], preferred_element_type=F32)
        later = as_bf16((behind == padded_starts[slot] + 1) & (within < lengths[slot] - 1))
        earlier += jnp.dot(later, piece_ref[:, channels:], preferred_element_type=F32)
    out_ref[:, :channels] = earlier.astype(BF16)
    out_ref[:, channels:] = both.astype(BF16)


def layer_norm(values, scales):
    centered = values - jnp.mean(values, axis=-1, keepdims=True)
    variance = jnp.mean(centered * centered, axis=-1, keepdims=True)
    return centered * lax.rsqrt(variance + 1e-05) * scales


def arrange(offsets, place_ref, mine_ref, other_ref, conv_ref, proj_ref):
    _, columns, part_rows, lanes = mine_ref.shape
    side = len(offsets)
    tiles = part_rows // 8
    core = lax.rem(place_ref[1], 2)
    own = lax.rem(place_ref[0], side)

    def fill(conv_part_ref, proj_part_ref):
        for index, offset in enumerate(offsets):
            row = lax.rem(own + offset + side, side)
            for column in range(columns):
                at = column * side + row
                block = conv_part_ref[index, column].astype(F32)
                conv_ref[pl.ds(pl.multiple_of(at * part_rows, 8), part_rows), :] = block
                block = proj_part_ref[index, column].astype(F32)
                for tile in range(tiles):
                    into = pl.ds(pl.multiple_of(at * 8, 8), 8)
                    piece = block[tile * 8 : (tile + 1) * 8]
                    proj_ref[into, tile * lanes : (tile + 1) * lanes] = piece

    @pl.when(core == 0)
    def _():
        fill(mine_ref, other_ref)

    @pl.when(core == 1)
    def _():
        fill(other_ref, mine_ref)


def depthwise(gated_ref, depth_ref, mixed_ref, lane, at):
    rows = mixed_ref.shape[0]
    taps = depth_ref.shape[0]
    span = 56
    lanes = slice(lane, lane + 128)
    for row in range(0, rows, span):
        near = gated_ref[row : row + span + 32, lanes]
        total = None
        for low in range(7, -1, -1):
            partial = None
            for high in range(0, 32, 8):
                tap = high + low - 1
                if 0 <= tap < taps:
                    weight = depth_ref[tap : tap + 1, at : at + 128]
                    term = near[high : high + span + 8] * weight
                    partial = term if partial is None else partial + term
            if total is None:
                total = partial
            else:
                total = partial + pltpu.roll(total, span + 7, 0)
        mixed_ref[row : row + span, at : at + 128] = total[:span]


def mix_kernel(
    node_count,
    offsets,
    place_ref,
    pair_ref,
    dest_ref,
    xs_ref,
    mine_ref,
    other_ref,
    first_ref,
    depth_ref,
    gain_ref,
    weight_ref,
    out_ref,
    conv_ref,
    proj_ref,
    normed_ref,
    held_ref,
    gated_ref,
    mixed_ref,
    sems,
):
    rows, width = normed_ref.shape
    steps, _, block, _ = held_ref.shape
    copies = []
    for step in range(steps):
        part = weight_ref.at[:, pl.ds(step * block, block), :]
        copies.append(pltpu.make_async_copy(part, held_ref.at[step], sems.at[step]))
    for copy in copies:
        copy.start()

    arrange(offsets, place_ref, mine_ref, other_ref, conv_ref, proj_ref)
    front = jnp.dot(xs_ref[...], conv_ref[...].astype(BF16), preferred_element_type=F32)
    front = jnp.maximum(front, 0.0).astype(BF16)
    projected = jnp.dot(front, proj_ref[...].astype(BF16), preferred_element_type=F32)
    projected = projected.astype(BF16).astype(F32)
    normed_ref[...] = layer_norm(projected, first_ref[...]).astype(BF16)

    for buffer in range(2):
        gated_ref[buffer, pl.ds(0, GAP), :] = jnp.zeros((GAP, block), F32)
        gated_ref[buffer, pl.ds(GAP + rows, GAP), :] = jnp.zeros((GAP, block), F32)
    contract = (((1,), (1,)), ((), ()))

    def multiply(step):
        copies[step].wait()
        value, gate = (
            lax.dot_general(
                normed_ref[...], held_ref[step, part], contract, preferred_element_type=F32
            )
            for part in range(2)
        )
        gated = (value * jax.nn.sigmoid(gate)).astype(BF16)
        gated_ref[step % 2, pl.ds(GAP, rows), :] = gated.astype(F32)

    multiply(0)
    for step in range(steps):
        if step + 1 < steps:
            multiply(step + 1)
        for lane in range(0, block, 128):
            depthwise(gated_ref.at[step % 2], depth_ref, mixed_ref, lane, step * block + lane)

    scaled = layer_norm(mixed_ref[...], gain_ref[...])
    encoded = (scaled * jax.nn.sigmoid(scaled)).astype(BF16)
    _, starts, _ = arriving(place_ref[0], pair_ref, dest_ref, node_count)
    shape = (out_ref.shape[0], rows)
    row_ids = iota(shape, 0)
    target = row_ids - GAP
    for start in starts:
        target += jnp.where(row_ids >= start, GAP, 0)
    chosen = as_bf16(iota(shape, 1) == target)
    out_ref[...] = jnp.dot(chosen, encoded, preferred_element_type=F32).astype(BF16)


SMEM = pl.BlockSpec(memory_space=pltpu.SMEM)
VMEM = pl.BlockSpec(memory_space=pltpu.VMEM)
ANY = pl.BlockSpec(memory_space=pl.ANY)


def params(mebibytes):
    return pltpu.CompilerParams(vmem_limit_bytes=mebibytes * 2**20)


def cost(flops, moved):
    return pl.CostEstimate(flops=flops, bytes_accessed=moved, transcendentals=0)


def body(
    frames,
    utt_pairs,
    utt_dest,
    conv_weight,
    proj_weight,
    point_weight,
    depth_weight,
    gain_first,
    gain_second,
):
    node_count = lax.axis_size("dp")
    position = lax.axis_index("fsdp")
    frame_count, channels = frames.shape
    pair_count = frame_count // 2
    utts = utt_pairs.shape[2]
    spacing = node_count // utts
    slot_rows = pair_count // 2
    width = proj_weight.shape[1]
    place = jnp.stack([lax.axis_index("dp"), position]).astype(jnp.int32)
    pair_table = utt_pairs[0].T
    dest_table = utt_dest[0].T
    rows = pair_count + (utts - 1) * GAP

    weight_rows = jnp.swapaxes(point_weight, 1, 2)
    weight_full = lax.all_gather(weight_rows, "fsdp", axis=1, tiled=True)

    pieces = pl.pallas_call(
        functools.partial(cut_kernel, node_count),
        out_shape=[jax.ShapeDtypeStruct((slot_rows, 2 * channels), BF16)] * utts,
        in_specs=[SMEM, SMEM, SMEM, VMEM],
        out_specs=[VMEM] * utts,
        compiler_params=params(10),
        cost_estimate=cost(4 * 10**9, 4 * 10**6),
        name="cut",
    )(place, pair_table, dest_table, frames)
    arrived = [pieces[0]]
    for slot in range(1, utts):
        arrived.append(shifted(pieces[slot], "dp", slot * spacing))

    side = 8
    y_groups = [[y * side + z for y in range(side)] for z in range(side)]
    copies = pl.pallas_call(
        own_kernel,
        out_shape=jax.ShapeDtypeStruct((side,) + conv_weight.shape, BF16),
        in_specs=[SMEM, VMEM, VMEM],
        out_specs=VMEM,
        compiler_params=params(4),
        cost_estimate=cost(10**5, 3 * 10**5),
        name="own",
    )(place, conv_weight, proj_weight)
    by_y = lax.all_to_all(copies, "dp", 0, 0, axis_index_groups=y_groups)
    by_y, _ = lax.optimization_barrier((by_y, pieces[1]))
    below = along_z(by_y, side, 3)
    above = along_z(by_y, side, -3)
    from_below = along_z(jnp.stack([by_y, above]), side, 1)
    from_above = along_z(jnp.stack([by_y, below, above]), side, -1)
    mine = jnp.concatenate([jnp.stack([by_y, below, above]), from_below, from_above])
    offsets = (0, -3, 3, -1, 2, 1, -2, 4)
    other = core_swapped(mine, "fsdp")
    packed = pl.pallas_call(
        functools.partial(pack_kernel, node_count),
        out_shape=jax.ShapeDtypeStruct((rows, 3 * channels), BF16),
        in_specs=[SMEM, SMEM, SMEM] + [VMEM] * utts,
        out_specs=VMEM,
        compiler_params=params(14),
        cost_estimate=cost(60 * 10**9, 160 * 10**6),
        name="pack",
    )(place, pair_table, dest_table, *arrived)
    steps = 4
    block = width // steps
    return pl.pallas_call(
        functools.partial(mix_kernel, node_count, offsets),
        out_shape=jax.ShapeDtypeStruct((pair_count, width), BF16),
        in_specs=[SMEM] * 3 + [VMEM] * 6 + [ANY],
        out_specs=VMEM,
        scratch_shapes=[
            pltpu.VMEM((3 * channels, channels), F32),
            pltpu.VMEM((channels, width), F32),
            pltpu.VMEM((rows, width), BF16),
            pltpu.VMEM((steps, 2, block, width), BF16),
            pltpu.VMEM((2, rows + 2 * GAP, block), F32),
            pltpu.VMEM((rows, width), F32),
            pltpu.SemaphoreType.DMA((steps,)),
        ],
        compiler_params=params(50),
        cost_estimate=cost(6 * 10**9, 14 * 10**6),
        name="mix",
    )(
        place,
        pair_table,
        dest_table,
        packed,
        mine,
        other,
        gain_first[None],
        depth_weight,
        gain_second[None],
        weight_full,
    )


def solution(mesh):
    in_specs = (
        P(("dp", "fsdp"), None),
        P("fsdp", None, None),
        P("fsdp", None, None),
        P("dp", None),
        P("dp", None),
        P(None, None, "fsdp"),
        P(),
        P(),
        P(),
    )
    out_specs = P(("dp", "fsdp"), None)
    return jax.shard_map(body, mesh=mesh, in_specs=in_specs, out_specs=out_specs, check_vma=False)
```

```python
import functools

import jax
import jax.numpy as jnp
from jax import lax
from jax.experimental import pallas as pl
from jax.experimental.pallas import tpu as pltpu
from jax.sharding import PartitionSpec as P

GAP = 16
SUBLANES = 8
BF16 = jnp.bfloat16
F32 = jnp.float32


def shifted(value, axis, steps):
    count = lax.axis_size(axis)
    pairs = [(source, (source + steps) % count) for source in range(count)]
    return lax.ppermute(value, axis, pairs)


def core_swapped(value, axis):
    count = lax.axis_size(axis)
    return lax.ppermute(value, axis, [(j, j ^ 1) for j in range(count)])


def along_z(value, side, steps):
    pairs = [
        (y * side + z, y * side + (z + steps) % side) for y in range(side) for z in range(side)
    ]
    return lax.ppermute(value, "dp", pairs)


def as_bf16(mask):
    return jnp.where(mask, 1.0, 0.0).astype(BF16)


def iota(shape, axis):
    return lax.broadcasted_iota(jnp.int32, shape, axis)


def arriving(own, pair_ref, dest_ref, node_count):
    utts = pair_ref.shape[0]
    spacing = node_count // utts
    sources, lengths = [], []
    for slot in range(utts):
        source = lax.rem(own + node_count - slot * spacing, node_count)
        length = jnp.int32(0)
        for utt in range(utts):
            length += jnp.where(dest_ref[utt, source] == own, pair_ref[utt, source], 0)
        sources.append(source)
        lengths.append(length)
    starts, padded_starts = [], []
    for slot in range(utts):
        start, padded_start = jnp.int32(0), jnp.int32(0)
        for other in range(utts):
            if other != slot:
                before = sources[other] < sources[slot]
                start += jnp.where(before, lengths[other], 0)
                padded_start += jnp.where(before, lengths[other] + GAP, 0)
        starts.append(start)
        padded_starts.append(padded_start)
    return lengths, starts, padded_starts


def own_kernel(place_ref, conv_ref, proj_ref, out_ref):
    copies, part_rows, lanes = out_ref.shape
    proj = proj_ref[...].astype(F32)
    tiles = [proj[:, at : at + lanes] for at in range(0, proj.shape[1], lanes)]
    is_conv = lax.rem(place_ref[1], 2) == 0
    chosen = jnp.where(is_conv, conv_ref[...].astype(F32), jnp.concatenate(tiles, axis=0))
    for copy in range(copies):
        out_ref[copy] = chosen.astype(BF16)


def cut_kernel(node_count, place_ref, pair_ref, dest_ref, frames_ref, *out_refs):
    own = place_ref[0]
    utts = len(out_refs)
    spacing = node_count // utts
    slot_rows = out_refs[0].shape[0]
    frame_count, channels = frames_ref.shape
    offset = jnp.int32(0)
    starts = [jnp.int32(0)] * utts
    for utt in range(utts):
        for slot in range(utts):
            target = lax.rem(own + slot * spacing, node_count)
            starts[slot] += jnp.where(dest_ref[utt, own] == target, offset, 0)
        offset += pair_ref[utt, own]
    shape = (slot_rows, frame_count)
    ahead = iota(shape, 1) - 2 * iota(shape, 0)
    for slot in range(utts):
        for parity in range(2):
            chosen = as_bf16(ahead == 2 * starts[slot] + parity)
            rows = jnp.dot(chosen, frames_ref[...], preferred_element_type=F32)
            out_refs[slot][:, parity * channels : (parity + 1) * channels] = rows.astype(BF16)


def pack_kernel(node_count, place_ref, pair_ref, dest_ref, *refs):
    piece_refs, out_ref = refs[:-1], refs[-1]
    rows = out_ref.shape[0]
    slot_rows, width = piece_refs[0].shape
    channels = width // 2
    lengths, _, padded_starts = arriving(place_ref[0], pair_ref, dest_ref, node_count)
    shape = (rows, slot_rows)
    line = iota(shape, 0)
    spread = (line & (SUBLANES - 1)) * (rows // SUBLANES) + (line >> 3)
    behind = spread - iota(shape, 1)
    within = iota(shape, 1)
    both = jnp.zeros((rows, width), F32)
    earlier = jnp.zeros((rows, channels), F32)
    for slot, piece_ref in enumerate(piece_refs):
        here = as_bf16((behind == padded_starts[slot]) & (within < lengths[slot]))
        both += jnp.dot(here, piece_ref[...], preferred_element_type=F32)
        later = as_bf16((behind == padded_starts[slot] + 1) & (within < lengths[slot] - 1))
        earlier += jnp.dot(later, piece_ref[:, channels:], preferred_element_type=F32)
    out_ref[:, :channels] = earlier.astype(BF16)
    out_ref[:, channels:] = both.astype(BF16)


def layer_norm(values, scales):
    centered = values - jnp.mean(values, axis=-1, keepdims=True)
    variance = jnp.mean(centered * centered, axis=-1, keepdims=True)
    return centered * lax.rsqrt(variance + 1e-05) * scales


def arrange(offsets, place_ref, mine_ref, other_ref, conv_ref, proj_ref):
    _, columns, part_rows, lanes = mine_ref.shape
    side = len(offsets)
    tiles = part_rows // 8
    core = lax.rem(place_ref[1], 2)
    own = lax.rem(place_ref[0], side)

    def fill(conv_part_ref, proj_part_ref):
        for index, offset in enumerate(offsets):
            row = lax.rem(own + offset + side, side)
            for column in range(columns):
                at = column * side + row
                block = conv_part_ref[index, column].astype(F32)
                conv_ref[pl.ds(pl.multiple_of(at * part_rows, 8), part_rows), :] = block
                block = proj_part_ref[index, column].astype(F32)
                for tile in range(tiles):
                    into = pl.ds(pl.multiple_of(at * 8, 8), 8)
                    piece = block[tile * 8 : (tile + 1) * 8]
                    proj_ref[into, tile * lanes : (tile + 1) * lanes] = piece

    @pl.when(core == 0)
    def _():
        fill(mine_ref, other_ref)

    @pl.when(core == 1)
    def _():
        fill(other_ref, mine_ref)


def depthwise(gated_ref, depth_ref, mixed_ref, lane, at):
    taps = depth_ref.shape[0]
    lines = mixed_ref.shape[0] // SUBLANES
    lanes = slice(lane, lane + 128)
    weights = [depth_ref[tap : tap + 1, at : at + 128] for tap in range(taps)]
    span = 10
    for line in range(0, lines, span):
        near = gated_ref[line : line + span + taps - 1, :, lanes]
        total = near[:span] * weights[0]
        for tap in range(1, taps):
            total += near[tap : tap + span] * weights[tap]
        rows = slice(line * SUBLANES, (line + span) * SUBLANES)
        mixed_ref[rows, at : at + 128] = total.reshape(span * SUBLANES, 128)


def mix_kernel(
    node_count,
    offsets,
    place_ref,
    pair_ref,
    dest_ref,
    xs_ref,
    mine_ref,
    other_ref,
    first_ref,
    depth_ref,
    gain_ref,
    weight_ref,
    out_ref,
    conv_ref,
    proj_ref,
    normed_ref,
    held_ref,
    gated_ref,
    mixed_ref,
    sems,
):
    rows, width = normed_ref.shape
    steps, _, block, _ = held_ref.shape
    copies = []
    for step in range(steps):
        part = weight_ref.at[:, pl.ds(step * block, block), :]
        copies.append(pltpu.make_async_copy(part, held_ref.at[step], sems.at[step]))
    for copy in copies:
        copy.start()

    arrange(offsets, place_ref, mine_ref, other_ref, conv_ref, proj_ref)
    front = jnp.dot(xs_ref[...], conv_ref[...].astype(BF16), preferred_element_type=F32)
    front = jnp.maximum(front, 0.0).astype(BF16)
    projected = jnp.dot(front, proj_ref[...].astype(BF16), preferred_element_type=F32)
    projected = projected.astype(BF16).astype(F32)
    normed_ref[...] = layer_norm(projected, first_ref[...]).astype(BF16)

    lines = rows // SUBLANES
    half = depth_ref.shape[0] // 2
    edge = iota((half, SUBLANES, block), 1)
    contract = (((1,), (1,)), ((), ()))

    def multiply(step):
        copies[step].wait()
        value, gate = (
            lax.dot_general(
                normed_ref[...], held_ref[step, part], contract, preferred_element_type=F32
            )
            for part in range(2)
        )
        gated = (value * jax.nn.sigmoid(gate)).astype(BF16)
        gated = gated.astype(F32).reshape(lines, SUBLANES, block)
        before = pltpu.roll(gated[lines - half :], 1, 1)
        after = pltpu.roll(gated[:half], SUBLANES - 1, 1)
        held = gated_ref.at[step % 2]
        held[:half] = jnp.where(edge > 0, before, 0.0)
        held[half : half + lines] = gated
        held[half + lines :] = jnp.where(edge < SUBLANES - 1, after, 0.0)

    multiply(0)
    for step in range(steps):
        if step + 1 < steps:
            multiply(step + 1)
        for lane in range(0, block, 128):
            depthwise(gated_ref.at[step % 2], depth_ref, mixed_ref, lane, step * block + lane)

    scaled = layer_norm(mixed_ref[...], gain_ref[...])
    encoded = (scaled * jax.nn.sigmoid(scaled)).astype(BF16)
    _, starts, _ = arriving(place_ref[0], pair_ref, dest_ref, node_count)
    row_ids = iota((out_ref.shape[0], 1), 0)
    target = row_ids - GAP
    for start in starts:
        target += jnp.where(row_ids >= start, GAP, 0)
    sublane = jnp.zeros_like(target)
    for turn in range(1, SUBLANES):
        sublane += jnp.where(target >= turn * lines, 1, 0)
    target = (target - sublane * lines) * SUBLANES + sublane
    chosen = as_bf16(iota((out_ref.shape[0], rows), 1) == target)
    out_ref[...] = jnp.dot(chosen, encoded, preferred_element_type=F32).astype(BF16)


SMEM = pl.BlockSpec(memory_space=pltpu.SMEM)
VMEM = pl.BlockSpec(memory_space=pltpu.VMEM)
ANY = pl.BlockSpec(memory_space=pl.ANY)


def params(mebibytes):
    return pltpu.CompilerParams(vmem_limit_bytes=mebibytes * 2**20)


def cost(flops, moved):
    return pl.CostEstimate(flops=flops, bytes_accessed=moved, transcendentals=0)


def body(
    frames,
    utt_pairs,
    utt_dest,
    conv_weight,
    proj_weight,
    point_weight,
    depth_weight,
    gain_first,
    gain_second,
):
    node_count = lax.axis_size("dp")
    position = lax.axis_index("fsdp")
    frame_count, channels = frames.shape
    pair_count = frame_count // 2
    utts = utt_pairs.shape[2]
    spacing = node_count // utts
    slot_rows = pair_count // 2
    width = proj_weight.shape[1]
    place = jnp.stack([lax.axis_index("dp"), position]).astype(jnp.int32)
    pair_table = utt_pairs[0].T
    dest_table = utt_dest[0].T
    rows = pair_count + (utts - 1) * GAP

    weight_rows = jnp.swapaxes(point_weight, 1, 2)
    weight_full = lax.all_gather(weight_rows, "fsdp", axis=1, tiled=True)

    pieces = pl.pallas_call(
        functools.partial(cut_kernel, node_count),
        out_shape=[jax.ShapeDtypeStruct((slot_rows, 2 * channels), BF16)] * utts,
        in_specs=[SMEM, SMEM, SMEM, VMEM],
        out_specs=[VMEM] * utts,
        compiler_params=params(10),
        cost_estimate=cost(4 * 10**9, 4 * 10**6),
        name="cut",
    )(place, pair_table, dest_table, frames)
    arrived = [pieces[0]]
    for slot in range(1, utts):
        arrived.append(shifted(pieces[slot], "dp", slot * spacing))

    side = 8
    y_groups = [[y * side + z for y in range(side)] for z in range(side)]
    copies = pl.pallas_call(
        own_kernel,
        out_shape=jax.ShapeDtypeStruct((side,) + conv_weight.shape, BF16),
        in_specs=[SMEM, VMEM, VMEM],
        out_specs=VMEM,
        compiler_params=params(4),
        cost_estimate=cost(10**5, 3 * 10**5),
        name="own",
    )(place, conv_weight, proj_weight)
    by_y = lax.all_to_all(copies, "dp", 0, 0, axis_index_groups=y_groups)
    by_y, _ = lax.optimization_barrier((by_y, pieces[1]))
    below = along_z(by_y, side, 3)
    above = along_z(by_y, side, -3)
    from_below = along_z(jnp.stack([by_y, above]), side, 1)
    from_above = along_z(jnp.stack([by_y, below, above]), side, -1)
    mine = jnp.concatenate([jnp.stack([by_y, below, above]), from_below, from_above])
    offsets = (0, -3, 3, -1, 2, 1, -2, 4)
    other = core_swapped(mine, "fsdp")
    packed = pl.pallas_call(
        functools.partial(pack_kernel, node_count),
        out_shape=jax.ShapeDtypeStruct((rows, 3 * channels), BF16),
        in_specs=[SMEM, SMEM, SMEM] + [VMEM] * utts,
        out_specs=VMEM,
        compiler_params=params(14),
        cost_estimate=cost(60 * 10**9, 160 * 10**6),
        name="pack",
    )(place, pair_table, dest_table, *arrived)
    steps = 6
    block = width // steps
    return pl.pallas_call(
        functools.partial(mix_kernel, node_count, offsets),
        out_shape=jax.ShapeDtypeStruct((pair_count, width), BF16),
        in_specs=[SMEM] * 3 + [VMEM] * 6 + [ANY],
        out_specs=VMEM,
        scratch_shapes=[
            pltpu.VMEM((3 * channels, channels), F32),
            pltpu.VMEM((channels, width), F32),
            pltpu.VMEM((rows, width), BF16),
            pltpu.VMEM((steps, 2, block, width), BF16),
            pltpu.VMEM((2, rows // SUBLANES + depth_weight.shape[0] - 1, SUBLANES, block), F32),
            pltpu.VMEM((rows, width), F32),
            pltpu.SemaphoreType.DMA((steps,)),
        ],
        compiler_params=params(50),
        cost_estimate=cost(6 * 10**9, 14 * 10**6),
        name="mix",
    )(
        place,
        pair_table,
        dest_table,
        packed,
        mine,
        other,
        gain_first[None],
        depth_weight,
        gain_second[None],
        weight_full,
    )


def solution(mesh):
    in_specs = (
        P(("dp", "fsdp"), None),
        P("fsdp", None, None),
        P("fsdp", None, None),
        P("dp", None),
        P("dp", None),
        P(None, None, "fsdp"),
        P(),
        P(),
        P(),
    )
    out_specs = P(("dp", "fsdp"), None)
    return jax.shard_map(body, mesh=mesh, in_specs=in_specs, out_specs=out_specs, check_vma=False)
```

```python
import functools

import jax
import jax.numpy as jnp
from jax import lax
from jax.experimental import pallas as pl
from jax.experimental.pallas import tpu as pltpu
from jax.sharding import PartitionSpec as P

GAP = 16
SUBLANES = 8
BF16 = jnp.bfloat16
F32 = jnp.float32


def shifted(value, axis, steps):
    count = lax.axis_size(axis)
    pairs = [(source, (source + steps) % count) for source in range(count)]
    return lax.ppermute(value, axis, pairs)


def core_swapped(value, axis):
    count = lax.axis_size(axis)
    return lax.ppermute(value, axis, [(j, j ^ 1) for j in range(count)])


def along_z(value, side, steps):
    pairs = [
        (y * side + z, y * side + (z + steps) % side) for y in range(side) for z in range(side)
    ]
    return lax.ppermute(value, "dp", pairs)


def as_bf16(mask):
    return jnp.where(mask, 1.0, 0.0).astype(BF16)


def iota(shape, axis):
    return lax.broadcasted_iota(jnp.int32, shape, axis)


def arriving(own, pair_ref, dest_ref, node_count):
    utts = pair_ref.shape[0]
    spacing = node_count // utts
    sources, lengths = [], []
    for slot in range(utts):
        source = lax.rem(own + node_count - slot * spacing, node_count)
        length = jnp.int32(0)
        for utt in range(utts):
            length += jnp.where(dest_ref[utt, source] == own, pair_ref[utt, source], 0)
        sources.append(source)
        lengths.append(length)
    starts, padded_starts = [], []
    for slot in range(utts):
        start, padded_start = jnp.int32(0), jnp.int32(0)
        for other in range(utts):
            if other != slot:
                before = sources[other] < sources[slot]
                start += jnp.where(before, lengths[other], 0)
                padded_start += jnp.where(before, lengths[other] + GAP, 0)
        starts.append(start)
        padded_starts.append(padded_start)
    return lengths, starts, padded_starts


def own_kernel(place_ref, conv_ref, proj_ref, out_ref):
    copies, part_rows, lanes = out_ref.shape
    proj = proj_ref[...].astype(F32)
    tiles = [proj[:, at : at + lanes] for at in range(0, proj.shape[1], lanes)]
    is_conv = lax.rem(place_ref[1], 2) == 0
    chosen = jnp.where(is_conv, conv_ref[...].astype(F32), jnp.concatenate(tiles, axis=0))
    for copy in range(copies):
        out_ref[copy] = chosen.astype(BF16)


def cut_kernel(node_count, place_ref, pair_ref, dest_ref, frames_ref, *out_refs):
    own = place_ref[0]
    utts = len(out_refs)
    spacing = node_count // utts
    slot_rows = out_refs[0].shape[0]
    frame_count, channels = frames_ref.shape
    offset = jnp.int32(0)
    starts = [jnp.int32(0)] * utts
    for utt in range(utts):
        for slot in range(utts):
            target = lax.rem(own + slot * spacing, node_count)
            starts[slot] += jnp.where(dest_ref[utt, own] == target, offset, 0)
        offset += pair_ref[utt, own]
    window = 2 * slot_rows + 16
    shape = (slot_rows, window)
    ahead = iota(shape, 1) - 2 * iota(shape, 0)
    for slot in range(utts):
        base = jnp.minimum((2 * starts[slot]) // 16 * 16, frame_count - window)
        near = frames_ref[pl.ds(pl.multiple_of(base, 16), window), :]
        for parity in range(2):
            chosen = as_bf16(ahead == 2 * starts[slot] - base + parity)
            rows = jnp.dot(chosen, near, preferred_element_type=F32)
            out_refs[slot][:, parity * channels : (parity + 1) * channels] = rows.astype(BF16)


def pack_kernel(node_count, place_ref, pair_ref, dest_ref, *refs):
    piece_refs, out_ref = refs[:-1], refs[-1]
    rows = out_ref.shape[0]
    slot_rows, width = piece_refs[0].shape
    channels = width // 2
    lengths, _, padded_starts = arriving(place_ref[0], pair_ref, dest_ref, node_count)
    shape = (rows, slot_rows)
    line = iota(shape, 0)
    spread = (line & (SUBLANES - 1)) * (rows // SUBLANES) + (line >> 3)
    behind = spread - iota(shape, 1)
    within = iota(shape, 1)
    lines = rows // SUBLANES
    place = iota((rows, 1), 0)
    place = (place & (SUBLANES - 1)) * lines + (place >> 3)
    both = jnp.zeros((rows, width), F32)
    filled = jnp.zeros((rows, 1), F32)
    for slot, piece_ref in enumerate(piece_refs):
        here = as_bf16((behind == padded_starts[slot]) & (within < lengths[slot]))
        both += jnp.dot(here, piece_ref[...], preferred_element_type=F32)
        since = place - padded_starts[slot]
        filled += jnp.where((since >= 0) & (since < lengths[slot]), 1.0, 0.0)
    odd = both[:, channels:].reshape(lines, SUBLANES, channels)
    first = pltpu.roll(odd[lines - 1 :], 1, 1)
    first = jnp.where(iota(first.shape, 1) > 0, first, 0.0)
    earlier = jnp.concatenate([first, odd[:-1]], axis=0).reshape(rows, channels)
    earlier = jnp.where(filled > 0.0, earlier, 0.0)
    out_ref[:, :channels] = earlier.astype(BF16)
    out_ref[:, channels:] = both.astype(BF16)


def layer_norm(values, scales):
    centered = values - jnp.mean(values, axis=-1, keepdims=True)
    variance = jnp.mean(centered * centered, axis=-1, keepdims=True)
    return centered * lax.rsqrt(variance + 1e-05) * scales


def arrange(offsets, place_ref, mine_ref, other_ref, conv_ref, proj_ref):
    _, columns, part_rows, lanes = mine_ref.shape
    side = len(offsets)
    tiles = part_rows // 8
    core = lax.rem(place_ref[1], 2)
    own = lax.rem(place_ref[0], side)

    def fill(conv_part_ref, proj_part_ref):
        for index, offset in enumerate(offsets):
            row = lax.rem(own + offset + side, side)
            for column in range(columns):
                at = column * side + row
                block = conv_part_ref[index, column].astype(F32)
                conv_ref[pl.ds(pl.multiple_of(at * part_rows, 8), part_rows), :] = block
                block = proj_part_ref[index, column].astype(F32)
                for tile in range(tiles):
                    into = pl.ds(pl.multiple_of(at * 8, 8), 8)
                    piece = block[tile * 8 : (tile + 1) * 8]
                    proj_ref[into, tile * lanes : (tile + 1) * lanes] = piece

    @pl.when(core == 0)
    def _():
        fill(mine_ref, other_ref)

    @pl.when(core == 1)
    def _():
        fill(other_ref, mine_ref)


def depthwise(gated_ref, depth_ref, mixed_ref, lane, at):
    taps = depth_ref.shape[0]
    lines = mixed_ref.shape[0] // SUBLANES
    lanes = slice(lane, lane + 128)
    weights = [depth_ref[tap : tap + 1, at : at + 128] for tap in range(taps)]
    span = 10
    for line in range(0, lines, span):
        near = gated_ref[line : line + span + taps - 1, :, lanes]
        total = near[:span] * weights[0]
        for tap in range(1, taps):
            total += near[tap : tap + span] * weights[tap]
        rows = slice(line * SUBLANES, (line + span) * SUBLANES)
        mixed_ref[rows, at : at + 128] = total.reshape(span * SUBLANES, 128)


def mix_kernel(
    node_count,
    offsets,
    place_ref,
    pair_ref,
    dest_ref,
    xs_ref,
    mine_ref,
    other_ref,
    first_ref,
    depth_ref,
    gain_ref,
    weight_ref,
    out_ref,
    conv_ref,
    proj_ref,
    normed_ref,
    held_ref,
    gated_ref,
    mixed_ref,
    sems,
):
    rows, width = normed_ref.shape
    steps, _, block, _ = held_ref.shape
    copies = []
    for step in range(steps):
        part = weight_ref.at[:, pl.ds(step * block, block), :]
        copies.append(pltpu.make_async_copy(part, held_ref.at[step], sems.at[step]))
    for copy in copies:
        copy.start()

    arrange(offsets, place_ref, mine_ref, other_ref, conv_ref, proj_ref)
    front = jnp.dot(xs_ref[...], conv_ref[...].astype(BF16), preferred_element_type=F32)
    front = jnp.maximum(front, 0.0).astype(BF16)
    projected = jnp.dot(front, proj_ref[...].astype(BF16), preferred_element_type=F32)
    projected = projected.astype(BF16).astype(F32)
    normed_ref[...] = layer_norm(projected, first_ref[...]).astype(BF16)

    lines = rows // SUBLANES
    half = depth_ref.shape[0] // 2
    edge = iota((half, SUBLANES, block), 1)
    contract = (((1,), (1,)), ((), ()))

    def multiply(step):
        copies[step].wait()
        value, gate = (
            lax.dot_general(
                normed_ref[...], held_ref[step, part], contract, preferred_element_type=F32
            )
            for part in range(2)
        )
        gated = (value * jax.nn.sigmoid(gate)).astype(BF16)
        gated = gated.astype(F32).reshape(lines, SUBLANES, block)
        before = pltpu.roll(gated[lines - half :], 1, 1)
        after = pltpu.roll(gated[:half], SUBLANES - 1, 1)
        held = gated_ref.at[step % 2]
        held[:half] = jnp.where(edge > 0, before, 0.0)
        held[half : half + lines] = gated
        held[half + lines :] = jnp.where(edge < SUBLANES - 1, after, 0.0)

    multiply(0)
    for step in range(steps):
        if step + 1 < steps:
            multiply(step + 1)
        for lane in range(0, block, 128):
            depthwise(gated_ref.at[step % 2], depth_ref, mixed_ref, lane, step * block + lane)

    scaled = layer_norm(mixed_ref[...], gain_ref[...])
    encoded = (scaled * jax.nn.sigmoid(scaled)).astype(BF16)
    _, starts, _ = arriving(place_ref[0], pair_ref, dest_ref, node_count)
    row_ids = iota((out_ref.shape[0], 1), 0)
    target = row_ids - GAP
    for start in starts:
        target += jnp.where(row_ids >= start, GAP, 0)
    sublane = jnp.zeros_like(target)
    for turn in range(1, SUBLANES):
        sublane += jnp.where(target >= turn * lines, 1, 0)
    target = (target - sublane * lines) * SUBLANES + sublane
    chosen = as_bf16(iota((out_ref.shape[0], rows), 1) == target)
    out_ref[...] = jnp.dot(chosen, encoded, preferred_element_type=F32).astype(BF16)


SMEM = pl.BlockSpec(memory_space=pltpu.SMEM)
VMEM = pl.BlockSpec(memory_space=pltpu.VMEM)
ANY = pl.BlockSpec(memory_space=pl.ANY)


def params(mebibytes):
    return pltpu.CompilerParams(vmem_limit_bytes=mebibytes * 2**20)


def cost(flops, moved):
    return pl.CostEstimate(flops=flops, bytes_accessed=moved, transcendentals=0)


def body(
    frames,
    utt_pairs,
    utt_dest,
    conv_weight,
    proj_weight,
    point_weight,
    depth_weight,
    gain_first,
    gain_second,
):
    node_count = lax.axis_size("dp")
    position = lax.axis_index("fsdp")
    frame_count, channels = frames.shape
    pair_count = frame_count // 2
    utts = utt_pairs.shape[2]
    spacing = node_count // utts
    slot_rows = pair_count // 2
    width = proj_weight.shape[1]
    place = jnp.stack([lax.axis_index("dp"), position]).astype(jnp.int32)
    pair_table = utt_pairs[0].T
    dest_table = utt_dest[0].T
    rows = pair_count + (utts - 1) * GAP

    weight_rows = jnp.swapaxes(point_weight, 1, 2)
    weight_full = lax.all_gather(weight_rows, "fsdp", axis=1, tiled=True)

    pieces = pl.pallas_call(
        functools.partial(cut_kernel, node_count),
        out_shape=[jax.ShapeDtypeStruct((slot_rows, 2 * channels), BF16)] * utts,
        in_specs=[SMEM, SMEM, SMEM, VMEM],
        out_specs=[VMEM] * utts,
        compiler_params=params(10),
        cost_estimate=cost(4 * 10**9, 4 * 10**6),
        name="cut",
    )(place, pair_table, dest_table, frames)
    arrived = [pieces[0]]
    for slot in range(1, utts):
        arrived.append(shifted(pieces[slot], "dp", slot * spacing))

    side = 8
    y_groups = [[y * side + z for y in range(side)] for z in range(side)]
    copies = pl.pallas_call(
        own_kernel,
        out_shape=jax.ShapeDtypeStruct((side,) + conv_weight.shape, BF16),
        in_specs=[SMEM, VMEM, VMEM],
        out_specs=VMEM,
        compiler_params=params(4),
        cost_estimate=cost(10**5, 3 * 10**5),
        name="own",
    )(place, conv_weight, proj_weight)
    by_y = lax.all_to_all(copies, "dp", 0, 0, axis_index_groups=y_groups)
    by_y, _ = lax.optimization_barrier((by_y, pieces[1]))
    below = along_z(by_y, side, 3)
    above = along_z(by_y, side, -3)
    from_below = along_z(jnp.stack([by_y, above]), side, 1)
    from_above = along_z(jnp.stack([by_y, below, above]), side, -1)
    mine = jnp.concatenate([jnp.stack([by_y, below, above]), from_below, from_above])
    offsets = (0, -3, 3, -1, 2, 1, -2, 4)
    other = core_swapped(mine, "fsdp")
    packed = pl.pallas_call(
        functools.partial(pack_kernel, node_count),
        out_shape=jax.ShapeDtypeStruct((rows, 3 * channels), BF16),
        in_specs=[SMEM, SMEM, SMEM] + [VMEM] * utts,
        out_specs=VMEM,
        compiler_params=params(14),
        cost_estimate=cost(60 * 10**9, 160 * 10**6),
        name="pack",
    )(place, pair_table, dest_table, *arrived)
    steps = 6
    block = width // steps
    return pl.pallas_call(
        functools.partial(mix_kernel, node_count, offsets),
        out_shape=jax.ShapeDtypeStruct((pair_count, width), BF16),
        in_specs=[SMEM] * 3 + [VMEM] * 6 + [ANY],
        out_specs=VMEM,
        scratch_shapes=[
            pltpu.VMEM((3 * channels, channels), F32),
            pltpu.VMEM((channels, width), F32),
            pltpu.VMEM((rows, width), BF16),
            pltpu.VMEM((steps, 2, block, width), BF16),
            pltpu.VMEM((2, rows // SUBLANES + depth_weight.shape[0] - 1, SUBLANES, block), F32),
            pltpu.VMEM((rows, width), F32),
            pltpu.SemaphoreType.DMA((steps,)),
        ],
        compiler_params=params(50),
        cost_estimate=cost(6 * 10**9, 14 * 10**6),
        name="mix",
    )(
        place,
        pair_table,
        dest_table,
        packed,
        mine,
        other,
        gain_first[None],
        depth_weight,
        gain_second[None],
        weight_full,
    )


def solution(mesh):
    in_specs = (
        P(("dp", "fsdp"), None),
        P("fsdp", None, None),
        P("fsdp", None, None),
        P("dp", None),
        P("dp", None),
        P(None, None, "fsdp"),
        P(),
        P(),
        P(),
    )
    out_specs = P(("dp", "fsdp"), None)
    return jax.shard_map(body, mesh=mesh, in_specs=in_specs, out_specs=out_specs, check_vma=False)
```

```python
import functools

import jax
import jax.numpy as jnp
from jax import lax
from jax.experimental import pallas as pl
from jax.experimental.pallas import tpu as pltpu
from jax.sharding import PartitionSpec as P

GAP = 16
SUBLANES = 8
BF16 = jnp.bfloat16
F32 = jnp.float32


def shifted(value, axis, steps):
    count = lax.axis_size(axis)
    pairs = [(source, (source + steps) % count) for source in range(count)]
    return lax.ppermute(value, axis, pairs)


def core_swapped(value, axis):
    count = lax.axis_size(axis)
    return lax.ppermute(value, axis, [(j, j ^ 1) for j in range(count)])


def along_z(value, side, steps):
    pairs = [
        (y * side + z, y * side + (z + steps) % side) for y in range(side) for z in range(side)
    ]
    return lax.ppermute(value, "dp", pairs)


def as_bf16(mask):
    return jnp.where(mask, 1.0, 0.0).astype(BF16)


def iota(shape, axis):
    return lax.broadcasted_iota(jnp.int32, shape, axis)


def arriving(own, pair_ref, dest_ref, node_count):
    utts = pair_ref.shape[0]
    spacing = node_count // utts
    sources, lengths = [], []
    for slot in range(utts):
        source = lax.rem(own + node_count - slot * spacing, node_count)
        length = jnp.int32(0)
        for utt in range(utts):
            length += jnp.where(dest_ref[utt, source] == own, pair_ref[utt, source], 0)
        sources.append(source)
        lengths.append(length)
    starts, padded_starts = [], []
    for slot in range(utts):
        start, padded_start = jnp.int32(0), jnp.int32(0)
        for other in range(utts):
            if other != slot:
                before = sources[other] < sources[slot]
                start += jnp.where(before, lengths[other], 0)
                padded_start += jnp.where(before, lengths[other] + GAP, 0)
        starts.append(start)
        padded_starts.append(padded_start)
    return lengths, starts, padded_starts


def own_kernel(place_ref, conv_ref, proj_ref, out_ref):
    copies, part_rows, lanes = out_ref.shape
    proj = proj_ref[...].astype(F32)
    tiles = [proj[:, at : at + lanes] for at in range(0, proj.shape[1], lanes)]
    is_conv = lax.rem(place_ref[1], 2) == 0
    chosen = jnp.where(is_conv, conv_ref[...].astype(F32), jnp.concatenate(tiles, axis=0))
    for copy in range(copies):
        out_ref[copy] = chosen.astype(BF16)


def cut_kernel(node_count, place_ref, pair_ref, dest_ref, frames_ref, *out_refs):
    own = place_ref[0]
    utts = len(out_refs)
    spacing = node_count // utts
    slot_rows = out_refs[0].shape[0]
    frame_count, channels = frames_ref.shape
    offset = jnp.int32(0)
    starts = [jnp.int32(0)] * utts
    for utt in range(utts):
        for slot in range(utts):
            target = lax.rem(own + slot * spacing, node_count)
            starts[slot] += jnp.where(dest_ref[utt, own] == target, offset, 0)
        offset += pair_ref[utt, own]
    window = 2 * slot_rows + 16
    shape = (slot_rows, window)
    ahead = iota(shape, 1) - 2 * iota(shape, 0)
    for slot in range(utts):
        base = jnp.minimum((2 * starts[slot]) // 16 * 16, frame_count - window)
        near = frames_ref[pl.ds(pl.multiple_of(base, 16), window), :]
        for parity in range(2):
            chosen = as_bf16(ahead == 2 * starts[slot] - base + parity)
            rows = jnp.dot(chosen, near, preferred_element_type=F32)
            out_refs[slot][:, parity * channels : (parity + 1) * channels] = rows.astype(BF16)


def pack_kernel(node_count, place_ref, pair_ref, dest_ref, *refs):
    piece_refs, out_ref = refs[:-1], refs[-1]
    rows = out_ref.shape[0]
    slot_rows, width = piece_refs[0].shape
    channels = width // 2
    lengths, _, padded_starts = arriving(place_ref[0], pair_ref, dest_ref, node_count)
    shape = (rows, slot_rows)
    line = iota(shape, 0)
    spread = (line & (SUBLANES - 1)) * (rows // SUBLANES) + (line >> 3)
    behind = spread - iota(shape, 1)
    within = iota(shape, 1)
    lines = rows // SUBLANES
    place = iota((rows, 1), 0)
    place = (place & (SUBLANES - 1)) * lines + (place >> 3)
    both = jnp.zeros((rows, width), F32)
    filled = jnp.zeros((rows, 1), F32)
    for slot, piece_ref in enumerate(piece_refs):
        here = as_bf16((behind == padded_starts[slot]) & (within < lengths[slot]))
        both += jnp.dot(here, piece_ref[...], preferred_element_type=F32)
        since = place - padded_starts[slot]
        filled += jnp.where((since >= 0) & (since < lengths[slot]), 1.0, 0.0)
    odd = both[:, channels:].reshape(lines, SUBLANES, channels)
    first = pltpu.roll(odd[lines - 1 :], 1, 1)
    first = jnp.where(iota(first.shape, 1) > 0, first, 0.0)
    earlier = jnp.concatenate([first, odd[:-1]], axis=0).reshape(rows, channels)
    earlier = jnp.where(filled > 0.0, earlier, 0.0)
    out_ref[:, :channels] = earlier.astype(BF16)
    out_ref[:, channels:] = both.astype(BF16)


def layer_norm(values, scales):
    centered = values - jnp.mean(values, axis=-1, keepdims=True)
    variance = jnp.mean(centered * centered, axis=-1, keepdims=True)
    return centered * lax.rsqrt(variance + 1e-05) * scales


def arrange(offsets, place_ref, mine_ref, other_ref, conv_ref, proj_ref):
    _, columns, part_rows, lanes = mine_ref.shape
    side = len(offsets)
    tiles = part_rows // 8
    core = lax.rem(place_ref[1], 2)
    own = lax.rem(place_ref[0], side)

    def fill(conv_part_ref, proj_part_ref):
        for index, offset in enumerate(offsets):
            row = lax.rem(own + offset + side, side)
            for column in range(columns):
                at = column * side + row
                block = conv_part_ref[index, column].astype(F32)
                conv_ref[pl.ds(pl.multiple_of(at * part_rows, 8), part_rows), :] = block
                block = proj_part_ref[index, column].astype(F32)
                for tile in range(tiles):
                    into = pl.ds(pl.multiple_of(at * 8, 8), 8)
                    piece = block[tile * 8 : (tile + 1) * 8]
                    proj_ref[into, tile * lanes : (tile + 1) * lanes] = piece

    @pl.when(core == 0)
    def _():
        fill(mine_ref, other_ref)

    @pl.when(core == 1)
    def _():
        fill(other_ref, mine_ref)


def depthwise(gated_ref, depth_ref, mixed_ref, lane, at):
    taps = depth_ref.shape[0]
    lines = mixed_ref.shape[0] // SUBLANES
    lanes = slice(lane, lane + 128)
    weights = [depth_ref[tap : tap + 1, at : at + 128] for tap in range(taps)]
    span = 7
    for line in range(0, lines, span):
        near = gated_ref[line : line + span + taps - 1, :, lanes]
        total = near[:span] * weights[0]
        for tap in range(1, taps):
            total += near[tap : tap + span] * weights[tap]
        rows = slice(line * SUBLANES, (line + span) * SUBLANES)
        mixed_ref[rows, at : at + 128] = total.reshape(span * SUBLANES, 128)


def mix_kernel(
    node_count,
    offsets,
    place_ref,
    pair_ref,
    dest_ref,
    xs_ref,
    mine_ref,
    other_ref,
    first_ref,
    depth_ref,
    gain_ref,
    weight_ref,
    out_ref,
    conv_ref,
    proj_ref,
    normed_ref,
    held_ref,
    gated_ref,
    mixed_ref,
    sems,
):
    rows, width = normed_ref.shape
    steps, _, block, _ = held_ref.shape
    copies = []
    for step in range(steps):
        part = weight_ref.at[:, pl.ds(step * block, block), :]
        copies.append(pltpu.make_async_copy(part, held_ref.at[step], sems.at[step]))
    for copy in copies:
        copy.start()

    arrange(offsets, place_ref, mine_ref, other_ref, conv_ref, proj_ref)
    front = jnp.dot(xs_ref[...], conv_ref[...].astype(BF16), preferred_element_type=F32)
    front = jnp.maximum(front, 0.0).astype(BF16)
    projected = jnp.dot(front, proj_ref[...].astype(BF16), preferred_element_type=F32)
    projected = projected.astype(BF16).astype(F32)
    normed_ref[...] = layer_norm(projected, first_ref[...]).astype(BF16)

    lines = rows // SUBLANES
    half = depth_ref.shape[0] // 2
    edge = iota((half, SUBLANES, block), 1)
    contract = (((1,), (1,)), ((), ()))

    def multiply(step):
        copies[step].wait()
        value, gate = (
            lax.dot_general(
                normed_ref[...], held_ref[step, part], contract, preferred_element_type=F32
            )
            for part in range(2)
        )
        gated = (value * jax.nn.sigmoid(gate)).astype(BF16)
        gated = gated.astype(F32).reshape(lines, SUBLANES, block)
        before = pltpu.roll(gated[lines - half :], 1, 1)
        after = pltpu.roll(gated[:half], SUBLANES - 1, 1)
        held = gated_ref.at[step % 2]
        held[:half] = jnp.where(edge > 0, before, 0.0)
        held[half : half + lines] = gated
        held[half + lines :] = jnp.where(edge < SUBLANES - 1, after, 0.0)

    multiply(0)
    for step in range(steps):
        if step + 1 < steps:
            multiply(step + 1)
        for lane in range(0, block, 128):
            depthwise(gated_ref.at[step % 2], depth_ref, mixed_ref, lane, step * block + lane)

    scaled = layer_norm(mixed_ref[...], gain_ref[...])
    encoded = (scaled * jax.nn.sigmoid(scaled)).astype(BF16)
    _, starts, _ = arriving(place_ref[0], pair_ref, dest_ref, node_count)
    row_ids = iota((out_ref.shape[0], 1), 0)
    target = row_ids - GAP
    for start in starts:
        target += jnp.where(row_ids >= start, GAP, 0)
    sublane = jnp.zeros_like(target)
    for turn in range(1, SUBLANES):
        sublane += jnp.where(target >= turn * lines, 1, 0)
    target = (target - sublane * lines) * SUBLANES + sublane
    chosen = as_bf16(iota((out_ref.shape[0], rows), 1) == target)
    out_ref[...] = jnp.dot(chosen, encoded, preferred_element_type=F32).astype(BF16)


SMEM = pl.BlockSpec(memory_space=pltpu.SMEM)
VMEM = pl.BlockSpec(memory_space=pltpu.VMEM)
ANY = pl.BlockSpec(memory_space=pl.ANY)


def params(mebibytes):
    return pltpu.CompilerParams(vmem_limit_bytes=mebibytes * 2**20)


def cost(flops, moved):
    return pl.CostEstimate(flops=flops, bytes_accessed=moved, transcendentals=0)


def body(
    frames,
    utt_pairs,
    utt_dest,
    conv_weight,
    proj_weight,
    point_weight,
    depth_weight,
    gain_first,
    gain_second,
):
    node_count = lax.axis_size("dp")
    position = lax.axis_index("fsdp")
    frame_count, channels = frames.shape
    pair_count = frame_count // 2
    utts = utt_pairs.shape[2]
    spacing = node_count // utts
    slot_rows = pair_count // 2
    width = proj_weight.shape[1]
    place = jnp.stack([lax.axis_index("dp"), position]).astype(jnp.int32)
    pair_table = utt_pairs[0].T
    dest_table = utt_dest[0].T
    rows = pair_count + (utts - 1) * GAP

    weight_rows = jnp.swapaxes(point_weight, 1, 2)
    weight_full = lax.all_gather(weight_rows, "fsdp", axis=1, tiled=True)

    pieces = pl.pallas_call(
        functools.partial(cut_kernel, node_count),
        out_shape=[jax.ShapeDtypeStruct((slot_rows, 2 * channels), BF16)] * utts,
        in_specs=[SMEM, SMEM, SMEM, VMEM],
        out_specs=[VMEM] * utts,
        compiler_params=params(10),
        cost_estimate=cost(4 * 10**9, 4 * 10**6),
        name="cut",
    )(place, pair_table, dest_table, frames)
    arrived = [pieces[0]]
    for slot in range(1, utts):
        arrived.append(shifted(pieces[slot], "dp", slot * spacing))

    side = 8
    y_groups = [[y * side + z for y in range(side)] for z in range(side)]
    copies = pl.pallas_call(
        own_kernel,
        out_shape=jax.ShapeDtypeStruct((side,) + conv_weight.shape, BF16),
        in_specs=[SMEM, VMEM, VMEM],
        out_specs=VMEM,
        compiler_params=params(4),
        cost_estimate=cost(10**5, 3 * 10**5),
        name="own",
    )(place, conv_weight, proj_weight)
    by_y = lax.all_to_all(copies, "dp", 0, 0, axis_index_groups=y_groups)
    by_y, _ = lax.optimization_barrier((by_y, pieces[1]))
    below = along_z(by_y, side, 3)
    above = along_z(by_y, side, -3)
    from_below = along_z(jnp.stack([by_y, above]), side, 1)
    from_above = along_z(jnp.stack([by_y, below, above]), side, -1)
    mine = jnp.concatenate([jnp.stack([by_y, below, above]), from_below, from_above])
    offsets = (0, -3, 3, -1, 2, 1, -2, 4)
    other = core_swapped(mine, "fsdp")
    packed = pl.pallas_call(
        functools.partial(pack_kernel, node_count),
        out_shape=jax.ShapeDtypeStruct((rows, 3 * channels), BF16),
        in_specs=[SMEM, SMEM, SMEM] + [VMEM] * utts,
        out_specs=VMEM,
        compiler_params=params(14),
        cost_estimate=cost(60 * 10**9, 160 * 10**6),
        name="pack",
    )(place, pair_table, dest_table, *arrived)
    steps = 6
    block = width // steps
    return pl.pallas_call(
        functools.partial(mix_kernel, node_count, offsets),
        out_shape=jax.ShapeDtypeStruct((pair_count, width), BF16),
        in_specs=[SMEM] * 3 + [VMEM] * 6 + [ANY],
        out_specs=VMEM,
        scratch_shapes=[
            pltpu.VMEM((3 * channels, channels), F32),
            pltpu.VMEM((channels, width), F32),
            pltpu.VMEM((rows, width), BF16),
            pltpu.VMEM((steps, 2, block, width), BF16),
            pltpu.VMEM((2, rows // SUBLANES + depth_weight.shape[0] - 1, SUBLANES, block), F32),
            pltpu.VMEM((rows, width), F32),
            pltpu.SemaphoreType.DMA((steps,)),
        ],
        compiler_params=params(50),
        cost_estimate=cost(6 * 10**9, 14 * 10**6),
        name="mix",
    )(
        place,
        pair_table,
        dest_table,
        packed,
        mine,
        other,
        gain_first[None],
        depth_weight,
        gain_second[None],
        weight_full,
    )


def solution(mesh):
    in_specs = (
        P(("dp", "fsdp"), None),
        P("fsdp", None, None),
        P("fsdp", None, None),
        P("dp", None),
        P("dp", None),
        P(None, None, "fsdp"),
        P(),
        P(),
        P(),
    )
    out_specs = P(("dp", "fsdp"), None)
    return jax.shard_map(body, mesh=mesh, in_specs=in_specs, out_specs=out_specs, check_vma=False)
```
